32 devices in a mesh: groups: 2 (over x), ctx: 16 (over z, y, core).
Axes of the slice: x: 2, y: 2, z: 4, core: 2. Of those that a mesh axis runs over, the one named last changes fastest.
Arguments:
- queries: bfloat16 [256, 16, 128], P(('groups', 'ctx')), parts along dimension 0
- new_keys: bfloat16 [256, 128], P(('groups', 'ctx')), parts along dimension 0
- new_values: bfloat16 [256, 128], P(('groups', 'ctx')), parts along dimension 0, may hold values from -6 to 6
- pool_keys: bfloat16 [384, 128, 128], P(('groups', 'ctx')), parts along dimension 0, may hold values from -6 to 6
- pool_values: bfloat16 [384, 128, 128], P(('groups', 'ctx')), parts along dimension 0, may hold values from -6 to 6
- block_owner: int32 [32, 12], P('groups'), parts along dimension 0, may hold values from 0 to 15, as said below
- block_id: int32 [32, 12], P('groups'), parts along dimension 0, may hold values from 0 to 11
- old_start: int32 [32, 12], P('groups'), parts along dimension 0, may hold values from 0 to 24575
- cached_counts: int32 [32], P('groups'), parts along dimension 0, may hold values from 1 to 12, 168 in all
Outputs:
- attended: bfloat16 [256, 16, 128], P(('groups', 'ctx')), parts along dimension 0
The draws below stay inside these ranges and needn't reach their ends.
There are 2 independent parts, one for each index of `groups`. The reference program is written for one: setup_inputs(seed, part) draws one part's arguments, and reference() takes and returns one part's arrays. A program takes and returns all parts, laid end to end along the dimension named above; each array names one. Nothing has to cross between parts.
Inputs may be any that keep to these rules, and one draw needn't show every extreme that they name: `block_owner`: row e lists the owners e, e + 1, ..., e + 12 - 1 modulo 16, each once, in a drawn order. `cached_counts`: entries sum to 168; entry e counts the slots of row e in use, always the first ones.
All inputs are finite; a program needn't handle non-finite values.
Results may differ from the reference program's by a relative error of at most 0.0109.
Values may be sent and summed in bfloat16 or wider, within the bound.
A program may use at most 64 MiB of HBM per device.

```python
import math
import jax
import jax.numpy as jnp
import numpy as np
from jax import lax

HEAD = 128
GROUP = 16
BLK = 128
NB = 12
NEW = 128
CACHE_BLOCKS = 192
OLD_SPAN = 24576
TOTAL_CACHED = 168
N_CTX = 16


def draw_block_owner(key, part):
    row_keys = jax.random.split(key, N_CTX)

    def one_row(row_key, row_index):
        order = jax.random.permutation(row_key, NB).astype(jnp.int32)
        return (row_index + order) % N_CTX
    return jax.vmap(one_row)(row_keys, jnp.arange(N_CTX, dtype=jnp.int32)).astype(jnp.int32)


def draw_queries(key, part):
    own_key = jax.random.fold_in(key, 1)
    values = jax.random.normal(own_key, (NEW, GROUP, HEAD), jnp.float32) * 3.25
    return jnp.clip(values, -16.0, 16.0).astype(jnp.bfloat16)


def draw_new_keys(key, part):
    own_key = jax.random.fold_in(key, 2)
    values = jax.random.normal(own_key, (NEW, HEAD), jnp.float32)
    return jnp.clip(values, -6.0, 6.0).astype(jnp.bfloat16)


def set_ends(entries, rng, least, high):
    longest = entries.shape.index(max(entries.shape))
    spots = []
    for shift in (0, 1):
        where = [jax.random.randint(jax.random.fold_in(rng, axis), (), 0, length) for axis, length in enumerate(entries.shape)]
        where[longest] = (where[longest] + shift) % entries.shape[longest]
        spots.append(tuple(where))
    return entries.at[spots[0]].set(least).at[spots[1]].set(high)


def shard_levels(stream_key, extent, shards, smallest, high):
    level = 1.0
    for axis_at, blocks in shards:
        draws = jax.random.uniform(jax.random.fold_in(jax.random.fold_in(stream_key, 6), axis_at), (blocks,), jnp.float32, smallest / len(shards), high / len(shards))
        level = level * jnp.repeat(jnp.exp(draws), extent[axis_at] // blocks).reshape((-1,) + (1,) * (len(extent) - 1 - axis_at))
    return level


def length_profile(number_of, total, limit, slope):
    portions = [(1 << 20) // math.isqrt(rank ** slope) + 1 for rank in range(2, number_of + 1)]
    rest, counts = total - limit - (number_of - 1), [1] * (number_of - 1)
    while rest > 0:
        free = [i for i in range(number_of - 1) if counts[i] < limit]
        whole, left = sum([portions[i] for i in free]), rest
        for i in free:
            extra = min(limit - counts[i], max(1, left * portions[i] // whole), rest)
            counts[i] = counts[i] + extra
            rest = rest - extra
    return np.array([limit] + counts)


def uneven(rng, amount, total, limit, lean):
    if amount == 2:
        one = jax.random.randint(rng, (), max(1, total - limit), min(limit, total - 1) + 1)
        return jnp.stack([one, total - one])
    tallies = jnp.asarray(length_profile(amount, total, limit, lean), jnp.int32)
    pairs = (amount - 1) // 2
    donor, receiver = tallies[1:1 + 2 * pairs:2], tallies[2:2 + 2 * pairs:2]
    room = jnp.minimum(donor - 1, limit - receiver)
    passed = jax.random.randint(jax.random.fold_in(rng, 1), (pairs,), 0, 1 << 20) % (room + 1)
    tallies = tallies.at[1:1 + 2 * pairs:2].set(donor - passed).at[2:2 + 2 * pairs:2].set(receiver + passed)
    return tallies[jax.random.permutation(jax.random.fold_in(rng, 2), amount)]


def noise(key, shape, width, limit, cuts=(), kind=jnp.bfloat16):
    drawn = width * jax.random.normal(key, shape, jnp.float32)
    if cuts:
        drawn = drawn * shard_levels(key, shape, cuts, -0.22, 0.18)
    return jnp.clip(drawn, -limit, limit).astype(kind)


def setup_inputs(seed: int = 0, part: int = 0) -> dict:
    splits = jax.random.split(jax.random.key(seed), 10)
    part_splits = jax.random.split(jax.random.fold_in(splits[9], part), 10)
    return {
        "queries": draw_queries(jax.random.fold_in(jax.random.fold_in(splits[9], part), 71), part),
        "new_keys": draw_new_keys(jax.random.fold_in(jax.random.fold_in(splits[9], part), 71), part),
        "new_values": noise(part_splits[2], (NEW, HEAD), 1.0, 6.0, ((0, 16),)),
        "pool_keys": noise(part_splits[3], (CACHE_BLOCKS, BLK, HEAD), 1.0, 6.0, ((0, 16),)),
        "pool_values": noise(part_splits[4], (CACHE_BLOCKS, BLK, HEAD), 1.0, 6.0, ((0, 16),)),
        "block_owner": draw_block_owner(jax.random.fold_in(jax.random.fold_in(splits[9], part), 71), part),
        "block_id": set_ends(jax.random.randint(part_splits[6], (N_CTX, NB), 0, NB), jax.random.fold_in(part_splits[6], 1), 0, NB - 1).astype(jnp.int32),
        "old_start": set_ends(jax.random.randint(part_splits[7], (N_CTX, NB), 0, OLD_SPAN), jax.random.fold_in(part_splits[7], 1), 0, OLD_SPAN - 1).astype(jnp.int32),
        "cached_counts": uneven(part_splits[8], N_CTX, TOTAL_CACHED, NB, 2).astype(jnp.int32),
    }


masked_score = -1e+30

def frequencies():
    pair_index = jnp.arange(HEAD // 2, dtype=jnp.float32)
    inverse = jnp.exp(-(2.0 * pair_index / HEAD) * math.log(500000.0))
    wavelen = 2.0 * math.pi / inverse
    smooth = (8192.0 / wavelen - 1.0) / 3.0
    blended = (1.0 - smooth) * inverse / 8.0 + smooth * inverse
    return jnp.where(wavelen > 8192.0, inverse / 8.0, jnp.where(wavelen < 2048.0, inverse, blended))

def rotate_blocks(block_keys, shift_by):
    angles = shift_by.astype(jnp.float32)[:, None, None] * frequencies()[None, None, :]
    cosine = jnp.cos(angles)
    sine_part = jnp.sin(angles)
    widened = block_keys.astype(jnp.float32)
    first_half = widened[..., :HEAD // 2]
    second_half = widened[..., HEAD // 2:]
    turned = jnp.concatenate([first_half * cosine - second_half * sine_part, second_half * cosine + first_half * sine_part], axis=-1)
    return turned.astype(jnp.bfloat16)

def reference(queries, new_keys, new_values, pool_keys, pool_values, block_owner, block_id, old_start, cached_counts):
    prefix = jnp.cumsum(cached_counts) - cached_counts
    new_start = BLK * (prefix[:, None] + jnp.arange(NB, dtype=jnp.int32)[None, :])
    shift_all = (new_start - old_start).astype(jnp.int32).reshape(-1)
    block_index = (block_owner * NB + block_id).reshape(-1).astype(jnp.int32)
    cached_keys = rotate_blocks(pool_keys[block_index], shift_all).reshape(-1, HEAD)
    cached_values = pool_values[block_index].reshape(-1, HEAD)
    block_live = jnp.arange(NB, dtype=jnp.int32)[None, :] < cached_counts[:, None]
    cached_live = jnp.repeat(block_live.reshape(-1), BLK)
    span_tokens = min(16, NEW)
    starts = jnp.arange(NEW // span_tokens, dtype=jnp.int32) * span_tokens
    score_scale = 1.0 / math.sqrt(HEAD)
    key_token = jnp.arange(NEW, dtype=jnp.int32)

    def attend_block(first_token):
        query_rows = lax.dynamic_slice_in_dim(queries, first_token, span_tokens, 0).reshape(span_tokens * GROUP, HEAD)
        cached = jnp.dot(query_rows, cached_keys.T, preferred_element_type=jnp.float32) * score_scale
        cached = jnp.where(cached_live[None, :], cached, masked_score)
        fresh_scores = jnp.dot(query_rows, new_keys.T, preferred_element_type=jnp.float32) * score_scale
        row_token = first_token + jnp.arange(span_tokens * GROUP, dtype=jnp.int32) // GROUP
        visible = key_token[None, :] <= row_token[:, None]
        fresh_scores = jnp.where(visible, fresh_scores, masked_score)
        row_max = jnp.maximum(lax.optimization_barrier(jnp.max(cached, axis=1)), lax.optimization_barrier(jnp.max(fresh_scores, axis=1)))
        cached_weights = jnp.where(cached_live[None, :], jnp.exp(cached - row_max[:, None]), 0.0)
        fresh_weights = jnp.where(visible, jnp.exp(fresh_scores - row_max[:, None]), 0.0)
        row_sum = lax.optimization_barrier(jnp.sum(cached_weights, axis=1)) + lax.optimization_barrier(jnp.sum(fresh_weights, axis=1))
        summed = jnp.dot(cached_weights.astype(jnp.bfloat16), cached_values, preferred_element_type=jnp.float32)
        summed = summed + jnp.dot(fresh_weights.astype(jnp.bfloat16), new_values, preferred_element_type=jnp.float32)
        return (summed / row_sum[:, None]).astype(jnp.bfloat16).reshape(span_tokens, GROUP, HEAD)
    return lax.map(attend_block, starts).reshape(NEW, GROUP, HEAD)
```

```python
import functools
import math

import jax
import jax.numpy as jnp
import numpy as np
from jax import lax
from jax.experimental import pallas as pl
from jax.experimental.pallas import tpu as pltpu
from jax.sharding import PartitionSpec as P

MESH = pl.DeviceIdType.MESH
NEG = -1e30
F32 = jnp.float32
BF16 = jnp.bfloat16


def frequencies(head):
    pair_index = np.arange(head // 2, dtype=np.float64)
    inverse = np.exp(-(2.0 * pair_index / head) * math.log(500000.0))
    wavelen = 2.0 * math.pi / inverse
    smooth = (8192.0 / wavelen - 1.0) / 3.0
    blended = (1.0 - smooth) * inverse / 8.0 + smooth * inverse
    freq = np.where(wavelen > 8192.0, inverse / 8.0, np.where(wavelen < 2048.0, inverse, blended))
    return np.tile(freq.astype(np.float32), (8, 2))


TAIL = 8


def pack(out_ref, r, out, lse):
    head, cols = out.shape
    hi = lse.astype(BF16).astype(F32)
    mid = (lse - hi).astype(BF16).astype(F32)
    low = lse - hi - mid
    row = lax.broadcasted_iota(jnp.int32, (TAIL, cols), 0)
    tail = jnp.where(row == 0, hi, jnp.where(row == 1, mid, jnp.where(row == 2, low, 0.0)))
    out_ref[r, 0:head] = out.astype(BF16)
    out_ref[r, head : head + TAIL] = tail.astype(BF16)


def unpack(ref, r, head):
    tail = ref[r, head : head + TAIL].astype(F32)
    lse = tail[0:1] + tail[1:2] + tail[2:3]
    return ref[r, 0:head].astype(F32), lse


def plan(nz):
    if nz == 4:
        return dict(
            greet=[(2, 0), (1, 0), (0, 1), (1, 1)],
            greet_inner=[(3, 0), (3, 1)],
            first=[(2, 0), (3, 0), (1, 0), (0, 1), (1, 1), (3, 1)],
            relay={(2, 0): [(1, 0), (1, 1), (0, 1)]},
            relay_inner=[(1, 0), (1, 1)],
            order=[(0, 0), (0, 1), (1, 0), (1, 1), (2, 0), (3, 0), (3, 1), (2, 1)],
            relay_at={3: [(2, 0)]},
            flush=[5],
        )
    far = [*range(2, nz), 1][: nz - 1]
    line = [(k, 0) for k in far]
    return dict(
        greet=line + [(0, 1)],
        greet_inner=[],
        first=line + [(0, 1)],
        relay={label: [(0, 1)] for label in line},
        relay_inner=[],
        order=[(0, 0)] + line + [(0, 1)] + [(k, 1) for k in far],
        relay_at={1: line},
        flush=[],
    )


def kernel(
    dims,
    q_ref,
    nk_ref,
    nv_ref,
    pk_ref,
    pv_ref,
    freq_ref,
    owner_hbm,
    id_hbm,
    old_hbm,
    count_hbm,
    o_ref,
    qbuf,
    pk_own,
    pv_own,
    pk_other,
    pv_other,
    nkbuf,
    nvbuf,
    fqbuf,
    kbuf,
    vbuf,
    sbuf,
    sbuf2,
    tbuf,
    tbuf2,
    wbuf,
    wbuf2,
    pbuf,
    outbuf,
    fbuf,
    owner_ref,
    id_ref,
    old_ref,
    count_ref,
    prefix,
    l_sem,
    q_recv,
    q_send,
    r_send,
    x_send,
    x_recv,
    f_send,
    f_recv,
):
    n, nb, blk, head, rows, fresh, group = dims
    ny = 2
    nz = n // (2 * ny)
    chips = n // 2
    me = lax.axis_index("ctx")
    grp = lax.axis_index("groups")
    c = lax.rem(me, 2)
    chip = me // 2
    y = lax.rem(chip, ny)
    z = chip // ny
    other = me + 1 - 2 * c
    todo = plan(nz)
    inner = jnp.logical_and(z > 0, z < nz - 1)

    def z_at(k):
        if nz & (nz - 1):
            return lax.rem(z + k, nz)
        total, bit = 0, 1
        while bit < nz:
            total = total + lax.rem(z // bit + k // bit, 2) * bit
            bit *= 2
        return total

    def chip_at(k, b):
        return z_at(k) * ny + lax.rem(y + b, ny)

    def maybe(only_inner, do):
        if only_inner:
            pl.when(inner)(do)
        else:
            do()

    barrier = pltpu.get_barrier_semaphore()

    def greet(to):
        pl.semaphore_signal(barrier, inc=1, device_id=(grp, to), device_id_type=MESH)

    for label in todo["greet"]:
        greet(2 * chip_at(*label) + c)
    for label in todo["greet_inner"]:
        maybe(True, lambda label=label: greet(2 * chip_at(*label) + c))
    greet(other)

    def load(i, src, dst):
        return pltpu.make_async_copy(src, dst, l_sem.at[i])

    load_small = [
        load(0, owner_hbm, owner_ref),
        load(1, id_hbm, id_ref),
        load(2, old_hbm, old_ref),
        load(3, count_hbm, count_ref),
        load(4, freq_ref, fqbuf),
    ]
    load_new = [
        load(5, q_ref, qbuf.at[chip]),
        load(6, nk_ref, nkbuf.at[0]),
        load(7, nv_ref, nvbuf.at[0]),
    ]
    load_pool = [load(8, pk_ref, pk_own), load(9, pv_ref, pv_own)]
    for d in load_small + load_new + load_pool:
        d.start()

    def copy(src, dst, ss, rs, to):
        return pltpu.make_async_remote_copy(
            src_ref=src, dst_ref=dst, send_sem=ss, recv_sem=rs,
            device_id=(grp, to), device_id_type=MESH,
        )

    def q_copy(slot, ss, to_chip):
        return copy(qbuf.at[slot], qbuf.at[slot], ss, q_recv.at[slot], 2 * to_chip + c)

    for d in load_small:
        d.wait()

    total = jnp.int32(0)
    for e in range(n):
        prefix[e] = total
        total = total + count_ref[e]

    pad = -(-nb // 8) * 8
    row = lax.broadcasted_iota(jnp.int32, (pad, head), 0)
    lane = lax.broadcasted_iota(jnp.int32, (pad, head), 1)

    def prepare(which, place, pkbuf, pvbuf):
        device = 2 * chip + which
        ids, dead = [], []
        shift = jnp.zeros((pad, head), jnp.int32)
        for i in range(nb):
            e = lax.rem(device - i + n, n)
            slot = jnp.int32(0)
            for j in range(1, nb):
                slot = jnp.where(owner_ref[e, j] == device, j, slot)
            ids.append(id_ref[e, slot])
            shift = jnp.where(row == i, blk * (prefix[e] + slot) - old_ref[e, slot], shift)
            dead.append(jnp.where(slot < count_ref[e], F32(0.0), F32(-NEG)))
        angles = shift.astype(F32) * fqbuf[0:1, :]
        cosine = jnp.cos(angles)
        sine = jnp.sin(angles)
        sine = jnp.where(lane < head // 2, -sine, sine)

        def fill():
            for i in range(nb):
                at = (place * nb + i) * blk
                x = pkbuf[ids[i]].astype(F32)
                turned = x * cosine[i : i + 1] + pltpu.roll(x, head // 2, 1) * sine[i : i + 1]
                kbuf[at : at + blk, :] = turned.astype(BF16)
                vbuf[0:head, at : at + blk] = pvbuf[ids[i]].T

        return dead, fill

    slots = 2 * nb
    vbuf[head : head + 16, :] = jnp.ones((16, slots * blk), BF16)
    dead_own, fill_own = prepare(c, 0, pk_own, pv_own)
    dead_other, fill_other = prepare(1 - c, 1, pk_other, pv_other)
    dead = dead_own + dead_other
    for d in load_new + load_pool:
        d.wait()
    fill_own()

    maybe_inner = todo["greet_inner"]
    pl.semaphore_wait(barrier, len(todo["greet"]) + 1 + jnp.where(inner, len(maybe_inner), 0))

    def send_own(label):
        return q_copy(chip, q_send.at[todo["first"].index(label)], chip_at(*label))

    for label in todo["first"]:
        maybe(label in maybe_inner, lambda label=label: send_own(label).start())
    shared = [
        copy(pk_own, pk_other, x_send.at[2], x_recv.at[2], other),
        copy(pv_own, pv_other, x_send.at[3], x_recv.at[3], other),
        copy(nkbuf.at[0], nkbuf.at[1], x_send.at[0], x_recv.at[0], other),
        copy(nvbuf.at[0], nvbuf.at[1], x_send.at[1], x_recv.at[1], other),
    ]
    for d in shared:
        d.start()

    def got(slot):
        q_copy(slot, q_send.at[0], chip).wait_recv()

    relays = [(src, to) for src in todo["relay"] for to in todo["relay"][src]]

    def relay_copy(src, to):
        return q_copy(chip_at(*src), r_send.at[relays.index((src, to))], chip_at(*to))

    def pass_on(src):
        got(chip_at(*src))
        for to in todo["relay"][src]:
            maybe(to in todo["relay_inner"], lambda to=to: relay_copy(src, to).start())

    for d in shared:
        d.wait_recv()
    fill_other()

    scale = math.log2(math.e) / math.sqrt(head)
    nt = (((1,), (1,)), ((), ()))
    new_k = jnp.concatenate([nkbuf[0].astype(F32), nkbuf[1].astype(F32)], axis=0).astype(BF16)
    new_v = jnp.concatenate([nvbuf[0].astype(F32), nvbuf[1].astype(F32)], axis=0)
    new_v = jnp.concatenate([new_v.T, jnp.ones((16, 2 * fresh), F32)], axis=0).astype(BF16)
    fresh_at = lax.broadcasted_iota(jnp.int32, (2 * fresh, rows), 0)
    fresh_at = jnp.where(
        fresh_at < fresh, me * fresh + fresh_at, other * fresh + fresh_at - fresh
    )
    token_at = lax.broadcasted_iota(jnp.int32, (2 * fresh, rows), 1) // group
    some = 4

    def attend(p, to, r, held):
        if to is not None:
            sb, tb, fb = to
            q = qbuf[p]
            fresh_s = lax.dot_general(new_k, q, nt, preferred_element_type=F32)
            visible = fresh_at <= (2 * p + c) * fresh + token_at
            fresh_s = jnp.where(visible, fresh_s, NEG)
            top = jnp.broadcast_to(jnp.max(fresh_s, axis=0, keepdims=True), (8, rows))
        if held is not None:
            hs, ht, hf = held
            was = ht[0:1, :]
        for i in range(0, slots, some):
            if to is not None:
                s = lax.dot_general(
                    kbuf[i * blk : (i + some) * blk, :], q, nt, preferred_element_type=F32
                )
                sb[i * blk : (i + some) * blk, :] = s
                for j in range(some):
                    part = s[j * blk : (j + 1) * blk].reshape(blk // 8, 8, rows)
                    top = jnp.maximum(top, jnp.max(part, axis=0) - dead[i + j])
            if held is not None:
                for j in range(i, i + some):
                    s = hs[j * blk : (j + 1) * blk, :]
                    w = jnp.exp2(s * scale - (was + dead[j]))
                    pbuf[j * blk : (j + 1) * blk, :] = w.astype(BF16)
        if held is not None:
            summed = jnp.dot(vbuf[...], pbuf[...], preferred_element_type=F32)
            summed = summed + jnp.dot(new_v, hf[...], preferred_element_type=F32)
            sums = summed[head : head + 1]
            some_live = sums > 0
            lse = jnp.where(some_live, was + jnp.log2(jnp.where(some_live, sums, 1.0)), NEG)
            pack(outbuf, r, summed[:head] * jnp.where(some_live, 1.0 / sums, 0.0), lse)
        if to is not None:
            top = jnp.max(top, axis=0, keepdims=True) * scale
            tb[...] = jnp.broadcast_to(top, (8, rows))
            fb[...] = jnp.where(visible, jnp.exp2(fresh_s * scale - top), 0.0).astype(BF16)

    def final_copy(r, p):
        return copy(outbuf.at[r], fbuf.at[chip], f_send.at[r], f_recv.at[chip], 2 * p + c)

    order = todo["order"]
    relayed = [order.index(src) for src in todo["relay"]]

    def chunk_at(r):
        if isinstance(r, int):
            return chip_at(*order[r])
        k, b = jnp.int32(0), jnp.int32(0)
        for i, (ki, bi) in enumerate(order):
            k = jnp.where(r == i, ki, k)
            b = jnp.where(r == i, bi, b)
        return chip_at(k, b)

    buffers = [(sbuf, tbuf, wbuf), (sbuf2, tbuf2, wbuf2)]

    def ready(r, p):
        if isinstance(r, int):
            if r not in relayed:
                got(p)
        else:
            @pl.when(r >= 1 + len(relayed))
            def _():
                got(p)

    def out(r):
        final_copy(r, chunk_at(r)).start()

    attend(chip, buffers[0], None, None)
    if chips <= 8:
        held = 0
        for r in range(1, chips):
            for src in todo["relay_at"].get(r, []):
                pass_on(src)
            if r in todo["flush"]:
                attend(None, None, held, buffers[held % 2])
                if held:
                    out(held)
                held = None
            p = chunk_at(r)
            ready(r, p)
            attend(p, buffers[r % 2], held, None if held is None else buffers[held % 2])
            if held:
                out(held)
            held = r
        attend(None, None, held, buffers[held % 2])
        out(held)
    else:
        for src in todo["relay_at"][1]:
            pass_on(src)

        def step(r, to, held):
            p = chunk_at(r)
            ready(r, p)
            attend(p, to, r - 1, held)

            @pl.when(r > 1)
            def _():
                out(r - 1)

        def two_steps(t, _):
            step(2 * t + 1, buffers[1], buffers[0])
            step(2 * t + 2, buffers[0], buffers[1])
            return 0

        lax.fori_loop(0, chips // 2 - 1, two_steps, 0)
        step(jnp.int32(chips - 1), buffers[1], buffers[0])
        attend(None, None, chips - 1, buffers[1])
        out(jnp.int32(chips - 1))

    acc, best = unpack(outbuf, 0, head)
    acc_sum = jnp.ones((1, rows), F32)
    for r in range(1, chips):
        src = chunk_at(r)
        copy(outbuf.at[0], fbuf.at[src], f_send.at[0], f_recv.at[src], other).wait_recv()
        part, lse = unpack(fbuf, src, head)
        new = jnp.maximum(best, lse)
        f_old = jnp.exp2(best - new)
        f = jnp.exp2(lse - new)
        acc = acc * f_old + part * f
        acc_sum = acc_sum * f_old + f
        best = new
    o_ref[...] = (acc / acc_sum).T.astype(BF16)

    for d in shared:
        d.wait_send()
    for label in todo["first"]:
        maybe(label in maybe_inner, lambda label=label: send_own(label).wait_send())
    for src, to in relays:
        maybe(to in todo["relay_inner"], lambda src=src, to=to: relay_copy(src, to).wait_send())
    for r in range(1, chips):
        final_copy(r, chip).wait_send()


def local(
    queries, new_keys, new_values, pool_keys, pool_values, block_owner, block_id, old_start,
    cached_counts,
):
    n, nb = block_owner.shape
    tokens, group, head = queries.shape
    blk = pool_keys.shape[1]
    fresh = new_keys.shape[0]
    rows = tokens * group
    chips = n // 2
    todo = plan(n // 4)
    vmem = pl.BlockSpec(memory_space=pltpu.VMEM)
    hbm = pl.BlockSpec(memory_space=pltpu.HBM)
    dma = pltpu.SemaphoreType.DMA
    keys = 2 * nb * blk
    out = pl.pallas_call(
        functools.partial(kernel, (n, nb, blk, head, rows, fresh, group)),
        out_shape=jax.ShapeDtypeStruct((rows, head), BF16),
        in_specs=[hbm] * 10,
        out_specs=vmem,
        scratch_shapes=[
            pltpu.VMEM((chips, rows, head), BF16),
            pltpu.VMEM((nb, blk, head), BF16),
            pltpu.VMEM((nb, blk, head), BF16),
            pltpu.VMEM((nb, blk, head), BF16),
            pltpu.VMEM((nb, blk, head), BF16),
            pltpu.VMEM((2, fresh, head), BF16),
            pltpu.VMEM((2, fresh, head), BF16),
            pltpu.VMEM((8, head), F32),
            pltpu.VMEM((keys, head), BF16),
            pltpu.VMEM((head + 16, keys), BF16),
            pltpu.VMEM((keys, rows), F32),
            pltpu.VMEM((keys, rows), F32),
            pltpu.VMEM((8, rows), F32),
            pltpu.VMEM((8, rows), F32),
            pltpu.VMEM((2 * fresh, rows), BF16),
            pltpu.VMEM((2 * fresh, rows), BF16),
            pltpu.VMEM((keys, rows), BF16),
            pltpu.VMEM((chips, head + TAIL, rows), BF16),
            pltpu.VMEM((chips, head + TAIL, rows), BF16),
            pltpu.SMEM(block_owner.shape, jnp.int32),
            pltpu.SMEM(block_id.shape, jnp.int32),
            pltpu.SMEM(old_start.shape, jnp.int32),
            pltpu.SMEM(cached_counts.shape, jnp.int32),
            pltpu.SMEM((n,), jnp.int32),
            dma((10,)),
            dma((chips,)),
            dma((len(todo["first"]),)),
            dma((sum(len(v) for v in todo["relay"].values()),)),
            dma((4,)),
            dma((4,)),
            dma((chips,)),
            dma((chips,)),
        ],
        compiler_params=pltpu.CompilerParams(
            collective_id=0, has_side_effects=True, vmem_limit_bytes=48 * 1024 * 1024
        ),
    )(*[pltpu.with_memory_space_constraint(v, pltpu.HBM) for v in (
        queries.reshape(rows, head), new_keys, new_values, pool_keys, pool_values,
        jnp.asarray(frequencies(head)), block_owner, block_id, old_start, cached_counts,
    )])
    return out.reshape(tokens, group, head)


def solution(mesh):
    placed = (
        P(("groups", "ctx"), None, None),
        P(("groups", "ctx"), None),
        P(("groups", "ctx"), None),
        P(("groups", "ctx"), None, None),
        P(("groups", "ctx"), None, None),
        P("groups", None),
        P("groups", None),
        P("groups", None),
        P("groups"),
    )
    return jax.shard_map(
        local,
        mesh=mesh,
        in_specs=placed,
        out_specs=P(("groups", "ctx"), None, None),
        check_vma=False,
    )
```

```python
import functools
import math

import jax
import jax.numpy as jnp
import numpy as np
from jax import lax
from jax.experimental import pallas as pl
from jax.experimental.pallas import tpu as pltpu
from jax.sharding import PartitionSpec as P

MESH = pl.DeviceIdType.MESH
NEG = -1e30
F32 = jnp.float32
BF16 = jnp.bfloat16


def frequencies(head):
    pair_index = np.arange(head // 2, dtype=np.float64)
    inverse = np.exp(-(2.0 * pair_index / head) * math.log(500000.0))
    wavelen = 2.0 * math.pi / inverse
    smooth = (8192.0 / wavelen - 1.0) / 3.0
    blended = (1.0 - smooth) * inverse / 8.0 + smooth * inverse
    freq = np.where(wavelen > 8192.0, inverse / 8.0, np.where(wavelen < 2048.0, inverse, blended))
    return np.tile(freq.astype(np.float32), (8, 2))


TAIL = 8


def pack(out_ref, r, out, lse):
    head, cols = out.shape
    hi = lse.astype(BF16).astype(F32)
    mid = (lse - hi).astype(BF16).astype(F32)
    low = lse - hi - mid
    row = lax.broadcasted_iota(jnp.int32, (TAIL, cols), 0)
    tail = jnp.where(row == 0, hi, jnp.where(row == 1, mid, jnp.where(row == 2, low, 0.0)))
    out_ref[r, 0:head] = out.astype(BF16)
    out_ref[r, head : head + TAIL] = tail.astype(BF16)


def unpack(ref, r, head):
    tail = ref[r, head : head + TAIL].astype(F32)
    lse = tail[0:1] + tail[1:2] + tail[2:3]
    return ref[r, 0:head].astype(F32), lse


def plan(nz):
    if nz == 4:
        return dict(
            greet=[(2, 0), (1, 0), (0, 1), (1, 1)],
            greet_inner=[(3, 0), (3, 1)],
            first=[(2, 0), (3, 0), (1, 0), (0, 1), (1, 1), (3, 1)],
            relay={(2, 0): [(1, 0), (1, 1), (0, 1)]},
            relay_inner=[(1, 0), (1, 1)],
            order=[(0, 0), (0, 1), (1, 0), (1, 1), (2, 0), (3, 1), (3, 0), (2, 1)],
            relay_at={3: [(2, 0)]},
            flush=[5],
            keep=[1, 2, 3],
            let_go=6,
        )
    far = [*range(2, nz), 1][: nz - 1]
    line = [(k, 0) for k in far]
    return dict(
        greet=line + [(0, 1)],
        greet_inner=[],
        first=line + [(0, 1)],
        relay={label: [(0, 1)] for label in line},
        relay_inner=[],
        order=[(0, 0)] + line + [(0, 1)] + [(k, 1) for k in far],
        relay_at={1: line},
        flush=[],
    )


def kernel(
    dims,
    q_ref,
    nk_ref,
    nv_ref,
    pk_ref,
    pv_ref,
    freq_ref,
    owner_hbm,
    id_hbm,
    old_hbm,
    count_hbm,
    o_ref,
    qbuf,
    pk_own,
    pv_own,
    pk_other,
    pv_other,
    nkbuf,
    nvbuf,
    fqbuf,
    kbuf,
    vbuf,
    sbuf,
    sbuf2,
    tbuf,
    tbuf2,
    wbuf,
    wbuf2,
    pbuf,
    outbuf,
    fbuf,
    owner_ref,
    id_ref,
    old_ref,
    count_ref,
    prefix,
    l_sem,
    q_recv,
    q_send,
    r_send,
    x_send,
    x_recv,
    f_send,
    f_recv,
):
    n, nb, blk, head, rows, fresh, group = dims
    ny = 2
    nz = n // (2 * ny)
    chips = n // 2
    me = lax.axis_index("ctx")
    grp = lax.axis_index("groups")
    c = lax.rem(me, 2)
    chip = me // 2
    y = lax.rem(chip, ny)
    z = chip // ny
    other = me + 1 - 2 * c
    todo = plan(nz)
    inner = jnp.logical_and(z > 0, z < nz - 1)

    def z_at(k):
        if nz & (nz - 1):
            return lax.rem(z + k, nz)
        total, bit = 0, 1
        while bit < nz:
            total = total + lax.rem(z // bit + k // bit, 2) * bit
            bit *= 2
        return total

    def chip_at(k, b):
        return z_at(k) * ny + lax.rem(y + b, ny)

    def maybe(only_inner, do):
        if only_inner:
            pl.when(inner)(do)
        else:
            do()

    barrier = pltpu.get_barrier_semaphore()

    def greet(to):
        pl.semaphore_signal(barrier, inc=1, device_id=(grp, to), device_id_type=MESH)

    for label in todo["greet"]:
        greet(2 * chip_at(*label) + c)
    for label in todo["greet_inner"]:
        maybe(True, lambda label=label: greet(2 * chip_at(*label) + c))
    greet(other)

    def load(i, src, dst):
        return pltpu.make_async_copy(src, dst, l_sem.at[i])

    load_small = [
        load(0, owner_hbm, owner_ref),
        load(1, id_hbm, id_ref),
        load(2, old_hbm, old_ref),
        load(3, count_hbm, count_ref),
        load(4, freq_ref, fqbuf),
    ]
    load_new = [
        load(5, q_ref, qbuf.at[chip]),
        load(6, nk_ref, nkbuf.at[0]),
        load(7, nv_ref, nvbuf.at[0]),
    ]
    load_pool = [load(8, pk_ref, pk_own), load(9, pv_ref, pv_own)]
    for d in load_small + load_new + load_pool:
        d.start()

    def copy(src, dst, ss, rs, to):
        return pltpu.make_async_remote_copy(
            src_ref=src, dst_ref=dst, send_sem=ss, recv_sem=rs,
            device_id=(grp, to), device_id_type=MESH,
        )

    def q_copy(slot, ss, to_chip):
        return copy(qbuf.at[slot], qbuf.at[slot], ss, q_recv.at[slot], 2 * to_chip + c)

    for d in load_small:
        d.wait()

    total = jnp.int32(0)
    for e in range(n):
        prefix[e] = total
        total = total + count_ref[e]

    pad = -(-nb // 8) * 8
    row = lax.broadcasted_iota(jnp.int32, (pad, head), 0)
    lane = lax.broadcasted_iota(jnp.int32, (pad, head), 1)

    def prepare(which, place, pkbuf, pvbuf):
        device = 2 * chip + which
        ids, dead = [], []
        shift = jnp.zeros((pad, head), jnp.int32)
        for i in range(nb):
            e = lax.rem(device - i + n, n)
            slot = jnp.int32(0)
            for j in range(1, nb):
                slot = jnp.where(owner_ref[e, j] == device, j, slot)
            ids.append(id_ref[e, slot])
            shift = jnp.where(row == i, blk * (prefix[e] + slot) - old_ref[e, slot], shift)
            dead.append(jnp.where(slot < count_ref[e], F32(0.0), F32(-NEG)))
        angles = shift.astype(F32) * fqbuf[0:1, :]
        cosine = jnp.cos(angles)
        sine = jnp.sin(angles)
        sine = jnp.where(lane < head // 2, -sine, sine)

        def fill():
            for i in range(nb):
                at = (place * nb + i) * blk
                x = pkbuf[ids[i]].astype(F32)
                turned = x * cosine[i : i + 1] + pltpu.roll(x, head // 2, 1) * sine[i : i + 1]
                kbuf[at : at + blk, :] = turned.astype(BF16)
                vbuf[0:head, at : at + blk] = pvbuf[ids[i]].T

        return dead, fill

    slots = 2 * nb
    vbuf[head : head + 16, :] = jnp.ones((16, slots * blk), BF16)
    dead_own, fill_own = prepare(c, 0, pk_own, pv_own)
    load_new[0].wait()

    maybe_inner = todo["greet_inner"]
    pl.semaphore_wait(barrier, len(todo["greet"]) + 1 + jnp.where(inner, len(maybe_inner), 0))

    def send_own(label):
        return q_copy(chip, q_send.at[todo["first"].index(label)], chip_at(*label))

    for label in todo["first"]:
        maybe(label in maybe_inner, lambda label=label: send_own(label).start())
    shared = [
        copy(pk_own, pk_other, x_send.at[2], x_recv.at[2], other),
        copy(pv_own, pv_other, x_send.at[3], x_recv.at[3], other),
        copy(nkbuf.at[0], nkbuf.at[1], x_send.at[0], x_recv.at[0], other),
        copy(nvbuf.at[0], nvbuf.at[1], x_send.at[1], x_recv.at[1], other),
    ]
    for d in load_new[1:] + load_pool:
        d.wait()
    for d in shared:
        d.start()
    fill_own()
    dead_other, fill_other = prepare(1 - c, 1, pk_other, pv_other)
    dead = dead_own + dead_other

    def got(slot):
        q_copy(slot, q_send.at[0], chip).wait_recv()

    relays = [(src, to) for src in todo["relay"] for to in todo["relay"][src]]

    def relay_copy(src, to):
        return q_copy(chip_at(*src), r_send.at[relays.index((src, to))], chip_at(*to))

    def pass_on(src):
        got(chip_at(*src))
        for to in todo["relay"][src]:
            maybe(to in todo["relay_inner"], lambda to=to: relay_copy(src, to).start())

    for d in shared:
        d.wait_recv()
    fill_other()

    scale = math.log2(math.e) / math.sqrt(head)
    nt = (((1,), (1,)), ((), ()))
    new_k = jnp.concatenate([nkbuf[0].astype(F32), nkbuf[1].astype(F32)], axis=0).astype(BF16)
    new_v = jnp.concatenate([nvbuf[0].astype(F32), nvbuf[1].astype(F32)], axis=0)
    new_v = jnp.concatenate([new_v.T, jnp.ones((16, 2 * fresh), F32)], axis=0).astype(BF16)
    fresh_at = lax.broadcasted_iota(jnp.int32, (2 * fresh, rows), 0)
    fresh_at = jnp.where(
        fresh_at < fresh, me * fresh + fresh_at, other * fresh + fresh_at - fresh
    )
    token_at = lax.broadcasted_iota(jnp.int32, (2 * fresh, rows), 1) // group
    some = 4

    def attend(p, to, r, held):
        if to is not None:
            sb, tb, fb = to
            q = qbuf[p]
            fresh_s = lax.dot_general(new_k, q, nt, preferred_element_type=F32)
            visible = fresh_at <= (2 * p + c) * fresh + token_at
            fresh_s = jnp.where(visible, fresh_s, NEG)
            top = jnp.broadcast_to(jnp.max(fresh_s, axis=0, keepdims=True), (8, rows))
        if held is not None:
            hs, ht, hf = held
            was = ht[0:1, :]
        for i in range(0, slots, some):
            if to is not None:
                s = lax.dot_general(
                    kbuf[i * blk : (i + some) * blk, :], q, nt, preferred_element_type=F32
                )
                sb[i * blk : (i + some) * blk, :] = s
                for j in range(some):
                    part = s[j * blk : (j + 1) * blk].reshape(blk // 8, 8, rows)
                    top = jnp.maximum(top, jnp.max(part, axis=0) - dead[i + j])
            if held is not None:
                for j in range(i, i + some):
                    s = hs[j * blk : (j + 1) * blk, :]
                    w = jnp.exp2(s * scale - (was + dead[j]))
                    pbuf[j * blk : (j + 1) * blk, :] = w.astype(BF16)
        if held is not None:
            summed = jnp.dot(vbuf[...], pbuf[...], preferred_element_type=F32)
            summed = summed + jnp.dot(new_v, hf[...], preferred_element_type=F32)
            sums = summed[head : head + 1]
            some_live = sums > 0
            lse = jnp.where(some_live, was + jnp.log2(jnp.where(some_live, sums, 1.0)), NEG)
            pack(outbuf, r, summed[:head] * jnp.where(some_live, 1.0 / sums, 0.0), lse)
        if to is not None:
            top = jnp.max(top, axis=0, keepdims=True) * scale
            tb[...] = jnp.broadcast_to(top, (8, rows))
            fb[...] = jnp.where(visible, jnp.exp2(fresh_s * scale - top), 0.0).astype(BF16)

    def final_copy(r, p):
        return copy(outbuf.at[r], fbuf.at[chip], f_send.at[r], f_recv.at[chip], 2 * p + c)

    order = todo["order"]
    relayed = [order.index(src) for src in todo["relay"]]

    def chunk_at(r):
        if isinstance(r, int):
            return chip_at(*order[r])
        k, b = jnp.int32(0), jnp.int32(0)
        for i, (ki, bi) in enumerate(order):
            k = jnp.where(r == i, ki, k)
            b = jnp.where(r == i, bi, b)
        return chip_at(k, b)

    buffers = [(sbuf, tbuf, wbuf), (sbuf2, tbuf2, wbuf2)]

    def ready(r, p):
        if isinstance(r, int):
            if r not in relayed:
                got(p)
        else:
            @pl.when(r >= 1 + len(relayed))
            def _():
                got(p)

    def out(r):
        final_copy(r, chunk_at(r)).start()

    attend(chip, buffers[0], None, None)
    if chips <= 8:
        held = 0
        kept = []
        for r in range(1, chips):
            for src in todo["relay_at"].get(r, []):
                pass_on(src)
            if r in todo["flush"]:
                attend(None, None, held, buffers[held % 2])
                if held:
                    out(held)
                held = None
            p = chunk_at(r)
            ready(r, p)
            attend(p, buffers[r % 2], held, None if held is None else buffers[held % 2])
            if held in todo["keep"]:
                kept.append(held)
            elif held:
                out(held)
            if r == todo["let_go"]:
                for h in kept:
                    out(h)
                kept = []
            held = r
        attend(None, None, held, buffers[held % 2])
        out(held)
    else:
        for src in todo["relay_at"][1]:
            pass_on(src)

        def step(r, to, held):
            p = chunk_at(r)
            ready(r, p)
            attend(p, to, r - 1, held)

            @pl.when(r > 1)
            def _():
                out(r - 1)

        def two_steps(t, _):
            step(2 * t + 1, buffers[1], buffers[0])
            step(2 * t + 2, buffers[0], buffers[1])
            return 0

        lax.fori_loop(0, chips // 2 - 1, two_steps, 0)
        step(jnp.int32(chips - 1), buffers[1], buffers[0])
        attend(None, None, chips - 1, buffers[1])
        out(jnp.int32(chips - 1))

    acc, best = unpack(outbuf, 0, head)
    acc_sum = jnp.ones((1, rows), F32)
    for r in range(1, chips):
        src = chunk_at(r)
        copy(outbuf.at[0], fbuf.at[src], f_send.at[0], f_recv.at[src], other).wait_recv()
        part, lse = unpack(fbuf, src, head)
        new = jnp.maximum(best, lse)
        f_old = jnp.exp2(best - new)
        f = jnp.exp2(lse - new)
        acc = acc * f_old + part * f
        acc_sum = acc_sum * f_old + f
        best = new
    o_ref[...] = (acc / acc_sum).T.astype(BF16)

    for d in shared:
        d.wait_send()
    for label in todo["first"]:
        maybe(label in maybe_inner, lambda label=label: send_own(label).wait_send())
    for src, to in relays:
        maybe(to in todo["relay_inner"], lambda src=src, to=to: relay_copy(src, to).wait_send())
    for r in range(1, chips):
        final_copy(r, chip).wait_send()


def local(
    queries, new_keys, new_values, pool_keys, pool_values, block_owner, block_id, old_start,
    cached_counts,
):
    n, nb = block_owner.shape
    tokens, group, head = queries.shape
    blk = pool_keys.shape[1]
    fresh = new_keys.shape[0]
    rows = tokens * group
    chips = n // 2
    todo = plan(n // 4)
    vmem = pl.BlockSpec(memory_space=pltpu.VMEM)
    hbm = pl.BlockSpec(memory_space=pltpu.HBM)
    dma = pltpu.SemaphoreType.DMA
    keys = 2 * nb * blk
    out = pl.pallas_call(
        functools.partial(kernel, (n, nb, blk, head, rows, fresh, group)),
        out_shape=jax.ShapeDtypeStruct((rows, head), BF16),
        in_specs=[hbm] * 10,
        out_specs=vmem,
        scratch_shapes=[
            pltpu.VMEM((chips, rows, head), BF16),
            pltpu.VMEM((nb, blk, head), BF16),
            pltpu.VMEM((nb, blk, head), BF16),
            pltpu.VMEM((nb, blk, head), BF16),
            pltpu.VMEM((nb, blk, head), BF16),
            pltpu.VMEM((2, fresh, head), BF16),
            pltpu.VMEM((2, fresh, head), BF16),
            pltpu.VMEM((8, head), F32),
            pltpu.VMEM((keys, head), BF16),
            pltpu.VMEM((head + 16, keys), BF16),
            pltpu.VMEM((keys, rows), F32),
            pltpu.VMEM((keys, rows), F32),
            pltpu.VMEM((8, rows), F32),
            pltpu.VMEM((8, rows), F32),
            pltpu.VMEM((2 * fresh, rows), BF16),
            pltpu.VMEM((2 * fresh, rows), BF16),
            pltpu.VMEM((keys, rows), BF16),
            pltpu.VMEM((chips, head + TAIL, rows), BF16),
            pltpu.VMEM((chips, head + TAIL, rows), BF16),
            pltpu.SMEM(block_owner.shape, jnp.int32),
            pltpu.SMEM(block_id.shape, jnp.int32),
            pltpu.SMEM(old_start.shape, jnp.int32),
            pltpu.SMEM(cached_counts.shape, jnp.int32),
            pltpu.SMEM((n,), jnp.int32),
            dma((10,)),
            dma((chips,)),
            dma((len(todo["first"]),)),
            dma((sum(len(v) for v in todo["relay"].values()),)),
            dma((4,)),
            dma((4,)),
            dma((chips,)),
            dma((chips,)),
        ],
        compiler_params=pltpu.CompilerParams(
            collective_id=0, has_side_effects=True, vmem_limit_bytes=48 * 1024 * 1024
        ),
    )(*[pltpu.with_memory_space_constraint(v, pltpu.HBM) for v in (
        queries.reshape(rows, head), new_keys, new_values, pool_keys, pool_values,
        jnp.asarray(frequencies(head)), block_owner, block_id, old_start, cached_counts,
    )])
    return out.reshape(tokens, group, head)


def solution(mesh):
    placed = (
        P(("groups", "ctx"), None, None),
        P(("groups", "ctx"), None),
        P(("groups", "ctx"), None),
        P(("groups", "ctx"), None, None),
        P(("groups", "ctx"), None, None),
        P("groups", None),
        P("groups", None),
        P("groups", None),
        P("groups"),
    )
    return jax.shard_map(
        local,
        mesh=mesh,
        in_specs=placed,
        out_specs=P(("groups", "ctx"), None, None),
        check_vma=False,
    )
```

```python
import functools
import math

import jax
import jax.numpy as jnp
import numpy as np
from jax import lax
from jax.experimental import pallas as pl
from jax.experimental.pallas import tpu as pltpu
from jax.sharding import PartitionSpec as P

MESH = pl.DeviceIdType.MESH
NEG = -1e30
F32 = jnp.float32
BF16 = jnp.bfloat16


def frequencies(head):
    pair_index = np.arange(head // 2, dtype=np.float64)
    inverse = np.exp(-(2.0 * pair_index / head) * math.log(500000.0))
    wavelen = 2.0 * math.pi / inverse
    smooth = (8192.0 / wavelen - 1.0) / 3.0
    blended = (1.0 - smooth) * inverse / 8.0 + smooth * inverse
    freq = np.where(wavelen > 8192.0, inverse / 8.0, np.where(wavelen < 2048.0, inverse, blended))
    return np.tile(freq.astype(np.float32), (8, 2))


TAIL = 8


def pack(out_ref, r, out, lse):
    head, cols = out.shape
    hi = lse.astype(BF16).astype(F32)
    mid = (lse - hi).astype(BF16).astype(F32)
    low = lse - hi - mid
    row = lax.broadcasted_iota(jnp.int32, (TAIL, cols), 0)
    tail = jnp.where(row == 0, hi, jnp.where(row == 1, mid, jnp.where(row == 2, low, 0.0)))
    out_ref[r, 0:head] = out.astype(BF16)
    out_ref[r, head : head + TAIL] = tail.astype(BF16)


def unpack(ref, r, head):
    tail = ref[r, head : head + TAIL].astype(F32)
    lse = tail[0:1] + tail[1:2] + tail[2:3]
    return ref[r, 0:head].astype(F32), lse


def plan(nz):
    if nz == 4:
        return dict(
            greet=[(2, 0), (1, 0), (0, 1), (1, 1)],
            greet_inner=[(3, 0), (3, 1)],
            first=[(2, 0), (3, 0), (1, 0), (0, 1), (1, 1), (3, 1)],
            relay={(2, 0): [(1, 0), (1, 1), (0, 1)]},
            relay_inner=[(1, 0), (1, 1)],
            order=[(0, 0), (0, 1), (1, 0), (1, 1), (2, 0), (3, 1), (3, 0), (2, 1)],
            relay_at={3: [(2, 0)]},
            flush=[5],
            keep=[1, 2, 3],
            let_go=6,
            by_y=[5, 6],
        )
    far = [*range(2, nz), 1][: nz - 1]
    line = [(k, 0) for k in far]
    return dict(
        greet=line + [(0, 1)],
        greet_inner=[],
        first=line + [(0, 1)],
        relay={label: [(0, 1)] for label in line},
        relay_inner=[],
        order=[(0, 0)] + line + [(0, 1)] + [(k, 1) for k in far],
        relay_at={1: line},
        flush=[],
        by_y=[],
    )


def kernel(
    dims,
    q_ref,
    nk_ref,
    nv_ref,
    pk_ref,
    pv_ref,
    freq_ref,
    owner_hbm,
    id_hbm,
    old_hbm,
    count_hbm,
    o_ref,
    qbuf,
    pk_own,
    pv_own,
    pk_other,
    pv_other,
    nkbuf,
    nvbuf,
    fqbuf,
    kbuf,
    vbuf,
    sbuf,
    sbuf2,
    tbuf,
    tbuf2,
    wbuf,
    wbuf2,
    pbuf,
    outbuf,
    fbuf,
    owner_ref,
    id_ref,
    old_ref,
    count_ref,
    prefix,
    l_sem,
    q_recv,
    q_send,
    r_send,
    x_send,
    x_recv,
    f_send,
    f_recv,
):
    n, nb, blk, head, rows, fresh, group = dims
    ny = 2
    nz = n // (2 * ny)
    chips = n // 2
    me = lax.axis_index("ctx")
    grp = lax.axis_index("groups")
    c = lax.rem(me, 2)
    chip = me // 2
    y = lax.rem(chip, ny)
    z = chip // ny
    other = me + 1 - 2 * c
    todo = plan(nz)
    inner = jnp.logical_and(z > 0, z < nz - 1)

    def z_at(k):
        if nz & (nz - 1):
            return lax.rem(z + k, nz)
        total, bit = 0, 1
        while bit < nz:
            total = total + lax.rem(z // bit + k // bit, 2) * bit
            bit *= 2
        return total

    def chip_at(k, b):
        return z_at(k) * ny + lax.rem(y + b, ny)

    def maybe(only_inner, do):
        if only_inner:
            pl.when(inner)(do)
        else:
            do()

    barrier = pltpu.get_barrier_semaphore()

    def greet(to):
        pl.semaphore_signal(barrier, inc=1, device_id=(grp, to), device_id_type=MESH)

    for label in todo["greet"]:
        greet(2 * chip_at(*label) + c)
    for label in todo["greet_inner"]:
        maybe(True, lambda label=label: greet(2 * chip_at(*label) + c))
    greet(other)

    def load(i, src, dst):
        return pltpu.make_async_copy(src, dst, l_sem.at[i])

    load_small = [
        load(0, owner_hbm, owner_ref),
        load(1, id_hbm, id_ref),
        load(2, old_hbm, old_ref),
        load(3, count_hbm, count_ref),
        load(4, freq_ref, fqbuf),
    ]
    load_new = [
        load(5, q_ref, qbuf.at[chip]),
        load(6, nk_ref, nkbuf.at[0]),
        load(7, nv_ref, nvbuf.at[0]),
    ]
    load_pool = [load(8, pk_ref, pk_own), load(9, pv_ref, pv_own)]
    for d in load_small + load_new + load_pool:
        d.start()

    def copy(src, dst, ss, rs, to):
        return pltpu.make_async_remote_copy(
            src_ref=src, dst_ref=dst, send_sem=ss, recv_sem=rs,
            device_id=(grp, to), device_id_type=MESH,
        )

    def q_copy(slot, ss, to_chip):
        return copy(qbuf.at[slot], qbuf.at[slot], ss, q_recv.at[slot], 2 * to_chip + c)

    for d in load_small:
        d.wait()

    total = jnp.int32(0)
    for e in range(n):
        prefix[e] = total
        total = total + count_ref[e]

    pad = -(-nb // 8) * 8
    row = lax.broadcasted_iota(jnp.int32, (pad, head), 0)
    lane = lax.broadcasted_iota(jnp.int32, (pad, head), 1)

    def prepare(which, place, pkbuf, pvbuf):
        device = 2 * chip + which
        ids, dead = [], []
        shift = jnp.zeros((pad, head), jnp.int32)
        for i in range(nb):
            e = lax.rem(device - i + n, n)
            slot = jnp.int32(0)
            for j in range(1, nb):
                slot = jnp.where(owner_ref[e, j] == device, j, slot)
            ids.append(id_ref[e, slot])
            shift = jnp.where(row == i, blk * (prefix[e] + slot) - old_ref[e, slot], shift)
            dead.append(jnp.where(slot < count_ref[e], F32(0.0), F32(-NEG)))
        angles = shift.astype(F32) * fqbuf[0:1, :]
        cosine = jnp.cos(angles)
        sine = jnp.sin(angles)
        sine = jnp.where(lane < head // 2, -sine, sine)

        def fill():
            for i in range(nb):
                at = (place * nb + i) * blk
                x = pkbuf[ids[i]].astype(F32)
                turned = x * cosine[i : i + 1] + pltpu.roll(x, head // 2, 1) * sine[i : i + 1]
                kbuf[at : at + blk, :] = turned.astype(BF16)
                vbuf[0:head, at : at + blk] = pvbuf[ids[i]].T

        return dead, fill

    slots = 2 * nb
    vbuf[head : head + 16, :] = jnp.ones((16, slots * blk), BF16)
    dead_own, fill_own = prepare(c, 0, pk_own, pv_own)
    load_new[0].wait()

    maybe_inner = todo["greet_inner"]
    pl.semaphore_wait(barrier, len(todo["greet"]) + 1 + jnp.where(inner, len(maybe_inner), 0))

    def send_own(label):
        return q_copy(chip, q_send.at[todo["first"].index(label)], chip_at(*label))

    for label in todo["first"]:
        maybe(label in maybe_inner, lambda label=label: send_own(label).start())
    shared = [
        copy(pk_own, pk_other, x_send.at[2], x_recv.at[2], other),
        copy(pv_own, pv_other, x_send.at[3], x_recv.at[3], other),
        copy(nkbuf.at[0], nkbuf.at[1], x_send.at[0], x_recv.at[0], other),
        copy(nvbuf.at[0], nvbuf.at[1], x_send.at[1], x_recv.at[1], other),
    ]
    for d in load_new[1:] + load_pool:
        d.wait()
    for d in shared:
        d.start()
    fill_own()
    dead_other, fill_other = prepare(1 - c, 1, pk_other, pv_other)
    dead = dead_own + dead_other

    def got(slot):
        q_copy(slot, q_send.at[0], chip).wait_recv()

    relays = [(src, to) for src in todo["relay"] for to in todo["relay"][src]]

    def relay_copy(src, to):
        return q_copy(chip_at(*src), r_send.at[relays.index((src, to))], chip_at(*to))

    def pass_on(src):
        got(chip_at(*src))
        for to in todo["relay"][src]:
            maybe(to in todo["relay_inner"], lambda to=to: relay_copy(src, to).start())

    for d in shared:
        d.wait_recv()
    fill_other()

    scale = math.log2(math.e) / math.sqrt(head)
    nt = (((1,), (1,)), ((), ()))
    new_k = jnp.concatenate([nkbuf[0].astype(F32), nkbuf[1].astype(F32)], axis=0).astype(BF16)
    new_v = jnp.concatenate([nvbuf[0].astype(F32), nvbuf[1].astype(F32)], axis=0)
    new_v = jnp.concatenate([new_v.T, jnp.ones((16, 2 * fresh), F32)], axis=0).astype(BF16)
    fresh_at = lax.broadcasted_iota(jnp.int32, (2 * fresh, rows), 0)
    fresh_at = jnp.where(
        fresh_at < fresh, me * fresh + fresh_at, other * fresh + fresh_at - fresh
    )
    token_at = lax.broadcasted_iota(jnp.int32, (2 * fresh, rows), 1) // group
    some = 4

    def attend(p, to, r, held):
        if to is not None:
            sb, tb, fb = to
            q = qbuf[p]
            fresh_s = lax.dot_general(new_k, q, nt, preferred_element_type=F32)
            visible = fresh_at <= (2 * p + c) * fresh + token_at
            fresh_s = jnp.where(visible, fresh_s, NEG)
            top = jnp.broadcast_to(jnp.max(fresh_s, axis=0, keepdims=True), (8, rows))
        if held is not None:
            hs, ht, hf = held
            was = ht[0:1, :]
        for i in range(0, slots, some):
            if to is not None:
                s = lax.dot_general(
                    kbuf[i * blk : (i + some) * blk, :], q, nt, preferred_element_type=F32
                )
                sb[i * blk : (i + some) * blk, :] = s
                for j in range(some):
                    part = s[j * blk : (j + 1) * blk].reshape(blk // 8, 8, rows)
                    top = jnp.maximum(top, jnp.max(part, axis=0) - dead[i + j])
            if held is not None:
                for j in range(i, i + some):
                    s = hs[j * blk : (j + 1) * blk, :]
                    w = jnp.exp2(s * scale - (was + dead[j]))
                    pbuf[j * blk : (j + 1) * blk, :] = w.astype(BF16)
        if held is not None:
            summed = jnp.dot(vbuf[...], pbuf[...], preferred_element_type=F32)
            summed = summed + jnp.dot(new_v, hf[...], preferred_element_type=F32)
            sums = summed[head : head + 1]
            some_live = sums > 0
            lse = jnp.where(some_live, was + jnp.log2(jnp.where(some_live, sums, 1.0)), NEG)
            pack(outbuf, r, summed[:head] * jnp.where(some_live, 1.0 / sums, 0.0), lse)
        if to is not None:
            top = jnp.max(top, axis=0, keepdims=True) * scale
            tb[...] = jnp.broadcast_to(top, (8, rows))
            fb[...] = jnp.where(visible, jnp.exp2(fresh_s * scale - top), 0.0).astype(BF16)

    def final_copy(r, p):
        return copy(outbuf.at[r], fbuf.at[chip], f_send.at[r], f_recv.at[chip], 2 * p + c)

    order = todo["order"]
    relayed = [order.index(src) for src in todo["relay"]]

    def chunk_at(r):
        if isinstance(r, int) and r in todo["by_y"]:
            return z_at(order[r][0]) * ny + todo["by_y"].index(r)
        if isinstance(r, int):
            return chip_at(*order[r])
        k, b = jnp.int32(0), jnp.int32(0)
        for i, (ki, bi) in enumerate(order):
            k = jnp.where(r == i, ki, k)
            b = jnp.where(r == i, bi, b)
        return chip_at(k, b)

    buffers = [(sbuf, tbuf, wbuf), (sbuf2, tbuf2, wbuf2)]

    def ready(r, p):
        if isinstance(r, int):
            if r not in relayed:
                got(p)
        else:
            @pl.when(r >= 1 + len(relayed))
            def _():
                got(p)

    def out(r):
        final_copy(r, chunk_at(r)).start()

    attend(chip, buffers[0], None, None)
    if chips <= 8:
        held = 0
        kept = []
        for r in range(1, chips):
            for src in todo["relay_at"].get(r, []):
                pass_on(src)
            if r in todo["flush"]:
                attend(None, None, held, buffers[held % 2])
                if held:
                    out(held)
                held = None
            p = chunk_at(r)
            ready(r, p)
            attend(p, buffers[r % 2], held, None if held is None else buffers[held % 2])
            if held in todo["keep"]:
                kept.append(held)
            elif held:
                out(held)
            if r == todo["let_go"]:
                for h in kept:
                    out(h)
                kept = []
            held = r
        attend(None, None, held, buffers[held % 2])
        out(held)
    else:
        for src in todo["relay_at"][1]:
            pass_on(src)

        def step(r, to, held):
            p = chunk_at(r)
            ready(r, p)
            attend(p, to, r - 1, held)

            @pl.when(r > 1)
            def _():
                out(r - 1)

        def two_steps(t, _):
            step(2 * t + 1, buffers[1], buffers[0])
            step(2 * t + 2, buffers[0], buffers[1])
            return 0

        lax.fori_loop(0, chips // 2 - 1, two_steps, 0)
        step(jnp.int32(chips - 1), buffers[1], buffers[0])
        attend(None, None, chips - 1, buffers[1])
        out(jnp.int32(chips - 1))

    acc, best = unpack(outbuf, 0, head)
    acc_sum = jnp.ones((1, rows), F32)
    for r in range(1, chips):
        src = chunk_at(r)
        copy(outbuf.at[0], fbuf.at[src], f_send.at[0], f_recv.at[src], other).wait_recv()
        part, lse = unpack(fbuf, src, head)
        new = jnp.maximum(best, lse)
        f_old = jnp.exp2(best - new)
        f = jnp.exp2(lse - new)
        acc = acc * f_old + part * f
        acc_sum = acc_sum * f_old + f
        best = new
    o_ref[...] = (acc / acc_sum).T.astype(BF16)

    for d in shared:
        d.wait_send()
    for label in todo["first"]:
        maybe(label in maybe_inner, lambda label=label: send_own(label).wait_send())
    for src, to in relays:
        maybe(to in todo["relay_inner"], lambda src=src, to=to: relay_copy(src, to).wait_send())
    for r in range(1, chips):
        final_copy(r, chip).wait_send()


def local(
    queries, new_keys, new_values, pool_keys, pool_values, block_owner, block_id, old_start,
    cached_counts,
):
    n, nb = block_owner.shape
    tokens, group, head = queries.shape
    blk = pool_keys.shape[1]
    fresh = new_keys.shape[0]
    rows = tokens * group
    chips = n // 2
    todo = plan(n // 4)
    vmem = pl.BlockSpec(memory_space=pltpu.VMEM)
    hbm = pl.BlockSpec(memory_space=pltpu.HBM)
    dma = pltpu.SemaphoreType.DMA
    keys = 2 * nb * blk
    out = pl.pallas_call(
        functools.partial(kernel, (n, nb, blk, head, rows, fresh, group)),
        out_shape=jax.ShapeDtypeStruct((rows, head), BF16),
        in_specs=[hbm] * 10,
        out_specs=vmem,
        scratch_shapes=[
            pltpu.VMEM((chips, rows, head), BF16),
            pltpu.VMEM((nb, blk, head), BF16),
            pltpu.VMEM((nb, blk, head), BF16),
            pltpu.VMEM((nb, blk, head), BF16),
            pltpu.VMEM((nb, blk, head), BF16),
            pltpu.VMEM((2, fresh, head), BF16),
            pltpu.VMEM((2, fresh, head), BF16),
            pltpu.VMEM((8, head), F32),
            pltpu.VMEM((keys, head), BF16),
            pltpu.VMEM((head + 16, keys), BF16),
            pltpu.VMEM((keys, rows), F32),
            pltpu.VMEM((keys, rows), F32),
            pltpu.VMEM((8, rows), F32),
            pltpu.VMEM((8, rows), F32),
            pltpu.VMEM((2 * fresh, rows), BF16),
            pltpu.VMEM((2 * fresh, rows), BF16),
            pltpu.VMEM((keys, rows), BF16),
            pltpu.VMEM((chips, head + TAIL, rows), BF16),
            pltpu.VMEM((chips, head + TAIL, rows), BF16),
            pltpu.SMEM(block_owner.shape, jnp.int32),
            pltpu.SMEM(block_id.shape, jnp.int32),
            pltpu.SMEM(old_start.shape, jnp.int32),
            pltpu.SMEM(cached_counts.shape, jnp.int32),
            pltpu.SMEM((n,), jnp.int32),
            dma((10,)),
            dma((chips,)),
            dma((len(todo["first"]),)),
            dma((sum(len(v) for v in todo["relay"].values()),)),
            dma((4,)),
            dma((4,)),
            dma((chips,)),
            dma((chips,)),
        ],
        compiler_params=pltpu.CompilerParams(
            collective_id=0, has_side_effects=True, vmem_limit_bytes=48 * 1024 * 1024
        ),
    )(*[pltpu.with_memory_space_constraint(v, pltpu.HBM) for v in (
        queries.reshape(rows, head), new_keys, new_values, pool_keys, pool_values,
        jnp.asarray(frequencies(head)), block_owner, block_id, old_start, cached_counts,
    )])
    return out.reshape(tokens, group, head)


def solution(mesh):
    placed = (
        P(("groups", "ctx"), None, None),
        P(("groups", "ctx"), None),
        P(("groups", "ctx"), None),
        P(("groups", "ctx"), None, None),
        P(("groups", "ctx"), None, None),
        P("groups", None),
        P("groups", None),
        P("groups", None),
        P("groups"),
    )
    return jax.shard_map(
        local,
        mesh=mesh,
        in_specs=placed,
        out_specs=P(("groups", "ctx"), None, None),
        check_vma=False,
    )
```
